32 devices in a mesh: dom: 8 (over y, x, core), seq: 4 (over z).
Axes of the slice: x: 2, y: 2, z: 4, core: 2. Of those that a mesh axis runs over, the one named last changes fastest.
Arguments:
- hidden: bfloat16 [8, 160, 3072], P('dom', 'seq'), may hold values from -6 to 6
- qkv: bfloat16 [8, 160, 12288], P('dom', 'seq'), may hold values from -10 to 10
- w_out: bfloat16 [4096, 3072], P('seq'), may hold values from -0.09375 to 0.09375
- gate: float32 [3072], replicated, may hold values from 2 to 6
- next_scale: float32 [3072], replicated, may hold values from -0.5 to 1.5
- ancestors: int32 [8], replicated, may hold values from 0 to 7, as said below
- w_next: bfloat16 [3072, 12288], P('dom', 'seq'), may hold values from -0.109375 to 0.109375
Outputs:
- next_hidden: bfloat16 [8, 160, 3072], P('dom', 'seq')
- next_qkv: bfloat16 [8, 160, 12288], P('dom', None, 'seq')
The draws below stay inside these ranges and needn't reach their ends.
Inputs may be any that keep to these rules, and one draw needn't show every extreme that they name: `ancestors`: at least one particle p continues particle p - 1, and at least one particle p continues particle p + 8 // 2 (both counted round).
All inputs are finite; a program needn't handle non-finite values.
Results may differ from the reference program's by a relative error of at most 0.017.
Values may be sent and summed in bfloat16 or wider, within the bound.
A program may use at most 64 MiB of HBM per device.

```python
import jax
import jax.numpy as jnp
from jax import lax

D = 3072
HEAD_DIM = 128
HEADS = 32
PARTICLES = 8
SEQ = 160
HD = 4096
N_SEQ = 4


def draw_qkv(key, part):
    shape = (PARTICLES, SEQ, HEADS, 3, HEAD_DIM)
    base = jnp.clip(jax.random.normal(key, shape, jnp.float32), -4.0, 4.0)
    return base.reshape(PARTICLES, SEQ, HEADS * 3 * HEAD_DIM).astype(jnp.bfloat16)


def draw_ancestors(key, part):
    first_key = jax.random.fold_in(key, 11)
    second_key = jax.random.fold_in(key, 23)
    label_key = jax.random.fold_in(key, 37)
    chosen_key = jax.random.fold_in(key, 41)
    first = jax.random.randint(first_key, (PARTICLES,), 0, PARTICLES, dtype=jnp.int32)
    second = jax.random.randint(second_key, (PARTICLES,), 0, PARTICLES, dtype=jnp.int32)
    ranked = jnp.minimum(first, second)
    labels = jax.random.permutation(label_key, PARTICLES).astype(jnp.int32)
    base = jnp.take(labels, ranked, axis=0).astype(jnp.int32)
    chosen = jax.random.randint(chosen_key, (), 0, PARTICLES, dtype=jnp.int32)
    before = ((chosen + PARTICLES - 1) % PARTICLES).astype(jnp.int32)
    opposite = ((chosen + PARTICLES // 2) % PARTICLES).astype(jnp.int32)
    positions = jnp.arange(PARTICLES, dtype=jnp.int32)
    result = jnp.where(positions == chosen, before, base).astype(jnp.int32)
    return jnp.where(positions == opposite, chosen, result).astype(jnp.int32)


def levels(own_key, shape, cuts, low, top_value):
    gain = 1.0
    for position, shards_of in cuts:
        heights = jax.random.uniform(jax.random.fold_in(jax.random.fold_in(own_key, 6), position), (shards_of,), jnp.float32, low / len(cuts), top_value / len(cuts))
        gain = gain * jnp.repeat(jnp.exp(heights), shape[position] // shards_of).reshape((-1,) + (1,) * (len(shape) - 1 - position))
    return gain


def gaussian(rng, dims, spread, most, cuts=(), kind=jnp.bfloat16):
    factor_of = levels(rng, dims, cuts, -0.22, 0.18) if cuts else 1.0
    drawn = jax.random.normal(rng, dims, jnp.float32) * spread * factor_of
    return jnp.minimum(jnp.maximum(drawn, -most), most).astype(kind)


def setup_inputs(seed: int = 0) -> dict:
    key_of = jax.random.split(jax.random.key(seed), 8)
    return {
        "hidden": gaussian(key_of[0], (PARTICLES, SEQ, D), 1.0, 6.0, ((0, 8), (1, 4))),
        "qkv": draw_qkv(jax.random.fold_in(key_of[7], 71), 0),
        "w_out": gaussian(key_of[2], (HD, D), HD ** -0.5, 0.09375, ((0, 4),)),
        "gate": jnp.clip(jax.random.uniform(key_of[3], (D,), jnp.float32, 2.0, 6.0), 2.0, 6.0),
        "next_scale": jnp.clip(jax.random.uniform(key_of[4], (D,), jnp.float32, -0.5, 1.5), -0.5, 1.5),
        "ancestors": draw_ancestors(jax.random.fold_in(key_of[7], 71), 0),
        "w_next": gaussian(key_of[6], (D, 3 * HD), D ** -0.5, 0.109375, ((0, 8), (1, 4))),
    }


def attend(block):
    layout = block.reshape(SEQ, HEADS, 3, HEAD_DIM).astype(jnp.float32)
    scores = jnp.einsum('qhd,khd->hqk', layout[:, :, 0], layout[:, :, 1]) * HEAD_DIM ** (-0.5)
    attn_weights = jax.nn.softmax(scores, axis=-1).astype(jnp.bfloat16)
    attn_weights = lax.optimization_barrier(attn_weights).astype(jnp.float32)
    attended = jnp.einsum('hqk,khd->qhd', attn_weights, layout[:, :, 2])
    return attended.astype(jnp.bfloat16).reshape(SEQ, HEADS * HEAD_DIM)

def block_update(hidden_rows, qkv_rows, w_out, gate):
    attended = attend(qkv_rows)
    group_cols = HEADS * HEAD_DIM // N_SEQ
    grouped = attended.reshape(SEQ, N_SEQ, group_cols).astype(jnp.float32)
    w_groups = w_out.reshape(N_SEQ, group_cols, D).astype(jnp.float32)
    partial_terms = jnp.einsum('sgc,gcd->gsd', grouped, w_groups)
    partial_terms = lax.optimization_barrier(partial_terms.astype(jnp.bfloat16)).astype(jnp.float32)
    branch = lax.optimization_barrier(jnp.sum(partial_terms, axis=0))
    return (hidden_rows.astype(jnp.float32) + gate * branch).astype(jnp.bfloat16)

def reference(hidden, qkv, w_out, gate, next_scale, ancestors, w_next):
    updated = lax.map(lambda both_rows: block_update(both_rows[0], both_rows[1], w_out, gate), (hidden, qkv))
    next_hidden = jnp.take(updated, ancestors.astype(jnp.int32), axis=0)
    widened = next_hidden.astype(jnp.float32)
    squares = lax.optimization_barrier(jnp.mean(widened * widened, axis=-1, keepdims=True))
    normed = (widened * lax.rsqrt(squares + 1e-06) * (1.0 + next_scale)).astype(jnp.bfloat16)
    next_qkv = lax.map(lambda normed_rows: jnp.dot(normed_rows, w_next, preferred_element_type=jnp.float32).astype(jnp.bfloat16), normed)
    return (next_hidden, next_qkv)
```

```python
import functools

import jax
import jax.numpy as jnp
from jax import lax
from jax.experimental import pallas as pl
from jax.experimental.pallas import tpu as pltpu
from jax.sharding import PartitionSpec as P

HEAD_DIM = 128
MESH = pl.DeviceIdType.MESH
F32 = jnp.float32
BF16 = jnp.bfloat16
OUT_CHUNKS = 2


def tile_of(width, most):
    return max(t for t in range(128, most + 1, 128) if width % t == 0)


def kernel(
    dom_n, seq_n,
    anc_ref, hidden_ref, qkv_ref, wout_ref, gate_ref, scale_ref, wnext_ref,
    nh_ref, out_ref,
    heads, wout_v, hid_v, att, part, rs_in, pieces, arrived, routed, landed,
    normed, act, w_all, acc,
    loc_sem, qs, qr, rs_s, rs_r, a_s, a_r, b_s, b_r, n_s, n_r,
    ring_s, ring_r, mate_s, mate_r, own_s, own_r,
):
    d = lax.axis_index("dom")
    s = lax.axis_index("seq")
    rows, width = hid_v.shape
    seq_len = seq_n * rows
    chips = dom_n // 2
    core = lax.rem(d, 2)
    mate = d + 1 - 2 * core
    chip = d // 2

    if chips % 2 == 0:
        half_n = chips // 2

        def chip_at(pos):
            back = pos // half_n
            return (1 - back) * 2 * pos + back * (2 * (chips - 1 - pos) + 1)

        pos = chip // 2 + lax.rem(chip, 2) * (chips - 1 - 2 * (chip // 2))
    else:
        def chip_at(pos):
            return pos

        pos = chip

    def at(offset):
        return chip_at(lax.rem(pos + offset + 2 * chips, chips))

    barrier = pltpu.get_barrier_semaphore()
    for k in range(1, seq_n):
        pl.semaphore_signal(barrier, inc=1, device_id=(d, lax.rem(s + k, seq_n)), device_id_type=MESH)
    for k in range(1, dom_n):
        pl.semaphore_signal(barrier, inc=1, device_id=(lax.rem(d + k, dom_n), s), device_id_type=MESH)
    pl.semaphore_wait(barrier, seq_n - 1 + dom_n - 1)

    def push(src, dst, send, recv, dev):
        return pltpu.make_async_remote_copy(
            src_ref=src, dst_ref=dst, send_sem=send, recv_sem=recv, device_id=dev, device_id_type=MESH
        )

    sent = []

    cols = heads.shape[2]
    q_copies = []
    order = sorted(range(1, seq_n), key=lambda k: -min(k, seq_n - k))
    for k in order:
        to = lax.rem(s + k, seq_n)
        c = push(
            qkv_ref.at[0, :, pl.ds(pl.multiple_of(to * cols, 128), cols)],
            heads.at[s], qs.at[k], qr.at[k], (d, to),
        )
        c.start()
        q_copies.append(c)
    sent += q_copies

    wrows = wnext_ref.shape[0]
    wcols = wnext_ref.shape[1] // 2

    def slot(half, owner):
        return w_all.at[half, pl.ds(pl.multiple_of(owner * wrows, 16), wrows), :]

    def ring(h, half):
        step = 1 if half == 0 else -1
        owner = 2 * at(-step * h) + core
        if h == 0:
            src = wnext_ref.at[:, pl.ds(half * wcols, wcols)]
        else:
            src = slot(half, owner)
        return push(
            src, slot(half, owner), ring_s.at[h, half], ring_r.at[h, half],
            (2 * at(step) + core, s),
        )

    def mate_copy(h, half):
        step = 1 if half == 0 else -1
        owner = 2 * at(-step * (h + 1)) + core
        return push(
            slot(half, owner), slot(half, owner), mate_s.at[h, half], mate_r.at[h, half], (mate, s)
        )

    hops = chips - 1
    ring_copies = {}
    mate_copies = {}

    def start_ring(h):
        for half in range(2):
            ring_copies[h, half] = ring(h, half)
            ring_copies[h, half].start()
            sent.append(ring_copies[h, half])

    def arrive(h):
        for half in range(2):
            ring_copies[h, half].wait_recv()

    def share(h):
        for half in range(2):
            mate_copies[h, half] = mate_copy(h, half)
            mate_copies[h, half].start()
            sent.append(mate_copies[h, half])

    if hops > 0:
        start_ring(0)
    own_copies = []
    local = []
    for half in range(2):
        src = wnext_ref.at[:, pl.ds(half * wcols, wcols)]
        c = push(src, slot(half, d), own_s.at[half], own_r.at[half], (mate, s))
        c.start()
        own_copies.append(c)
    sent += own_copies

    def keep(src, dst, i):
        c = pltpu.make_async_copy(src, dst, loc_sem.at[i])
        c.start()
        return c

    own_heads = keep(qkv_ref.at[0, :, pl.ds(pl.multiple_of(s * cols, 128), cols)], heads.at[s], 0)
    wout_copy = keep(wout_ref, wout_v, 1)
    hid_copy = keep(hidden_ref.at[0], hid_v, 2)
    own_w = [
        keep(wnext_ref.at[:, pl.ds(half * wcols, wcols)], slot(half, d), 3 + half) for half in range(2)
    ]

    own_heads.wait()
    for c in q_copies:
        c.wait_recv()

    done_hop = 0
    if hops > 0:
        arrive(0)
        if hops > 1:
            start_ring(1)
        share(0)

    head_n = cols // (3 * HEAD_DIM)

    def merge(x):
        return x.astype(F32).reshape(seq_len, x.shape[-1]).astype(BF16)

    def one_head(h, carry):
        base = pl.multiple_of(h * 3 * HEAD_DIM, HEAD_DIM)
        q = merge(heads[:, :, pl.ds(base, HEAD_DIM)])
        key = merge(heads[:, :, pl.ds(pl.multiple_of(base + HEAD_DIM, HEAD_DIM), HEAD_DIM)])
        v = merge(heads[:, :, pl.ds(pl.multiple_of(base + 2 * HEAD_DIM, HEAD_DIM), HEAD_DIM)])
        sc = lax.dot_general(q, key, (((1,), (1,)), ((), ())), preferred_element_type=F32)
        sc = sc * HEAD_DIM ** (-0.5)
        e = jnp.exp(sc - jnp.max(sc, axis=-1, keepdims=True))
        w = (e / jnp.sum(e, axis=-1, keepdims=True)).astype(BF16)
        o = jnp.dot(w, v, preferred_element_type=F32).astype(BF16)
        att[:, pl.ds(pl.multiple_of(h * HEAD_DIM, HEAD_DIM), HEAD_DIM)] = o
        return carry

    lax.fori_loop(0, head_n, one_head, 0)
    wout_copy.wait()

    chunk = width // OUT_CHUNKS
    tile = tile_of(chunk, 512)
    rs_copies = []
    for n in range(OUT_CHUNKS):
        def project(t, carry, n=n):
            c0 = pl.ds(pl.multiple_of(n * chunk + t * tile, 128), tile)
            y = jnp.dot(att[...], wout_v[:, c0], preferred_element_type=F32)
            part[:, :, c0] = y.reshape(seq_n, rows, tile).astype(BF16)
            return carry

        lax.fori_loop(0, chunk // tile, project, 0)
        for k in order:
            to = lax.rem(s + k, seq_n)
            c = push(
                part.at[to, :, pl.ds(n * chunk, chunk)], rs_in.at[s, :, pl.ds(n * chunk, chunk)],
                rs_s.at[n, k], rs_r.at[n, k], (d, to),
            )
            c.start()
            rs_copies.append(c)
    sent += rs_copies
    hid_copy.wait()

    if hops > 1:
        arrive(1)
        share(1)
    for c in rs_copies:
        c.wait_recv()

    piece = width // dom_n
    for j in range(dom_n):
        c0 = slice(j * piece, (j + 1) * piece)
        total = part[s, :, c0].astype(F32)
        for k in range(1, seq_n):
            total = total + rs_in[lax.rem(s + k, seq_n), :, c0].astype(F32)
        pieces[j] = (hid_v[:, c0].astype(F32) + gate_ref[:, c0] * total).astype(BF16)

    a_copies = []
    for k in range(1, dom_n):
        to = lax.rem(d + k, dom_n)
        c = push(pieces.at[to], arrived.at[d], a_s.at[k], a_r.at[k], (to, s))
        c.start()
        a_copies.append(c)
    sent += a_copies
    arrived[d] = pieces[d]
    for c in a_copies:
        c.wait_recv()
    for p in range(dom_n):
        routed[p] = arrived[anc_ref[p]]
    b_copies = []
    for k in range(1, dom_n):
        to = lax.rem(d + k, dom_n)
        c = push(routed.at[to], landed.at[d], b_s.at[k], b_r.at[k], (to, s))
        c.start()
        b_copies.append(c)
    sent += b_copies
    landed[d] = routed[d]
    for c in b_copies:
        c.wait_recv()
    if hops > 2:
        start_ring(2)

    squares = jnp.zeros((rows, 1), F32)
    for j in range(dom_n):
        x = landed[j]
        nh_ref[0, :, j * piece:(j + 1) * piece] = x
        x = x.astype(F32)
        squares = squares + jnp.sum(x * x, axis=-1, keepdims=True)
    inv = lax.rsqrt(squares / width + 1e-06)
    for j in range(dom_n):
        c0 = slice(j * piece, (j + 1) * piece)
        normed[s, :, c0] = (landed[j].astype(F32) * inv * (1.0 + scale_ref[:, c0])).astype(BF16)
    n_copies = []
    for k in order:
        to = lax.rem(s + k, seq_n)
        c = push(normed.at[s], normed.at[s], n_s.at[k], n_r.at[k], (d, to))
        c.start()
        n_copies.append(c)
    sent += n_copies
    for c in own_w:
        c.wait()
    for c in own_copies:
        c.wait_recv()
    for c in n_copies:
        c.wait_recv()
    act[...] = merge(normed[...])

    wide = tile_of(wcols, 512)
    steps = wcols // wide
    aligned = wrows % 128 == 0

    def add(half, owner, first, last):
        k0 = pl.multiple_of(owner * wrows, 128)

        def body(t, carry):
            c0 = pl.ds(pl.multiple_of(t * wide, 128), wide)
            o0 = pl.ds(pl.multiple_of(half * wcols + t * wide, 128), wide)
            y = jnp.dot(
                act[:, pl.ds(k0, wrows)], w_all[half, pl.ds(k0, wrows), c0],
                preferred_element_type=F32,
            )
            if not first:
                y = y + acc[:, o0]
            if last:
                out_ref[0, :, o0] = y.astype(BF16)
            else:
                acc[:, o0] = y
            return carry

        lax.fori_loop(0, steps, body, 0)

    if aligned:
        for half in range(2):
            add(half, d, True, False)
            add(half, mate, False, hops == 0)
    for h in range(hops):
        if h > 1:
            arrive(h)
            if h + 1 < hops:
                start_ring(h + 1)
            share(h)
        last = h == hops - 1
        for half in range(2):
            step = 1 if half == 0 else -1
            if aligned:
                add(half, 2 * at(-step * (h + 1)) + core, False, False)
        for half in range(2):
            step = 1 if half == 0 else -1
            mate_copies[h, half].wait_recv()
            if aligned:
                add(half, 2 * at(-step * (h + 1)) + 1 - core, False, last)
    if not aligned:
        for half in range(2):
            def whole(t, carry, half=half):
                c0 = pl.ds(pl.multiple_of(t * wide, 128), wide)
                o0 = pl.ds(pl.multiple_of(half * wcols + t * wide, 128), wide)
                y = jnp.dot(act[...], w_all[half, :, c0], preferred_element_type=F32)
                out_ref[0, :, o0] = y.astype(BF16)
                return carry

            lax.fori_loop(0, steps, whole, 0)
    for c in sent:
        c.wait_send()


def body(dom_n, seq_n, hidden, qkv, w_out, gate, next_scale, ancestors, w_next):
    _, rows, width = hidden.shape
    cols = qkv.shape[2] // seq_n
    seq_len = rows * seq_n
    out_cols = w_next.shape[1]
    att_cols = w_out.shape[0]
    hops = max(dom_n // 2 - 1, 1)
    piece = width // dom_n
    sem = pltpu.SemaphoreType.DMA
    any_spec = pl.BlockSpec(memory_space=pl.ANY)
    vmem = pl.BlockSpec(memory_space=pltpu.VMEM)
    return pl.pallas_call(
        functools.partial(kernel, dom_n, seq_n),
        out_shape=(
            jax.ShapeDtypeStruct((1, rows, width), BF16),
            jax.ShapeDtypeStruct((1, seq_len, out_cols), BF16),
        ),
        in_specs=[
            pl.BlockSpec(memory_space=pltpu.SMEM), any_spec, any_spec, any_spec, vmem, vmem, any_spec,
        ],
        out_specs=(vmem, vmem),
        scratch_shapes=[
            pltpu.VMEM((seq_n, rows, cols), BF16),
            pltpu.VMEM((att_cols, width), BF16),
            pltpu.VMEM((rows, width), BF16),
            pltpu.VMEM((seq_len, att_cols), BF16),
            pltpu.VMEM((seq_n, rows, width), BF16),
            pltpu.VMEM((seq_n, rows, width), BF16),
            pltpu.VMEM((dom_n, rows, piece), BF16),
            pltpu.VMEM((dom_n, rows, piece), BF16),
            pltpu.VMEM((dom_n, rows, piece), BF16),
            pltpu.VMEM((dom_n, rows, piece), BF16),
            pltpu.VMEM((seq_n, rows, width), BF16),
            pltpu.VMEM((seq_len, width), BF16),
            pltpu.VMEM((2, width, out_cols // 2), BF16),
            pltpu.VMEM((seq_len, out_cols), F32),
            sem((5,)),
            sem((seq_n,)), sem((seq_n,)),
            sem((OUT_CHUNKS, seq_n)), sem((OUT_CHUNKS, seq_n)),
            sem((dom_n,)), sem((dom_n,)),
            sem((dom_n,)), sem((dom_n,)),
            sem((seq_n,)), sem((seq_n,)),
            sem((hops, 2)), sem((hops, 2)),
            sem((hops, 2)), sem((hops, 2)),
            sem((2,)), sem((2,)),
        ],
        compiler_params=pltpu.CompilerParams(
            collective_id=0, has_side_effects=True, vmem_limit_bytes=60 * 1024 * 1024
        ),
    )(ancestors, hidden, qkv, w_out, gate[None], next_scale[None], w_next)


def solution(mesh):
    in_specs = (
        P("dom", "seq", None),
        P("dom", "seq", None),
        P("seq", None),
        P(),
        P(),
        P(),
        P("dom", "seq"),
    )
    out_specs = (P("dom", "seq", None), P("dom", None, "seq"))
    return jax.shard_map(
        functools.partial(body, mesh.shape["dom"], mesh.shape["seq"]),
        mesh=mesh, in_specs=in_specs, out_specs=out_specs, check_vma=False,
    )
```
